1024 devices in a mesh: section: 16 (over y, x), expert: 64 (over z, core).
Axes of the slice: x: 4, y: 4, z: 32, core: 2. Of those that a mesh axis runs over, the one named last changes fastest.
Arguments:
- forward_sent: bfloat16 [16, 4096, 2048], P('section', 'expert'), may hold values from -6 to 6
- embedded: bfloat16 [4096, 2048], P('expert'), may hold values from -6 to 6
- forward_routes: int32 [16, 4096, 2], P('section', 'expert'), may hold values from 0 to 63, all different within a row; in each aligned block of 64 rows (0 to 63, 64 to 127, ..., all dimensions but the last counted through in order) at most 3 rows name the same one
- backward_sent: bfloat16 [16, 4096, 2048], P('section', 'expert'), may hold values from -6 to 6
- loss_gradient: bfloat16 [4096, 2048], P('expert'), may hold values from -6 to 6
- saved_inputs: bfloat16 [16, 4096, 2048], P('section', 'expert'), may hold values from -6 to 6
- backward_routes: int32 [16, 4096, 2], P('section', 'expert'), may hold values from 0 to 63, all different within a row; in each aligned block of 64 rows (0 to 63, 64 to 127, ..., all dimensions but the last counted through in order) at most 3 rows name the same one
- pre_activation: bfloat16 [16, 64, 64, 3, 1024], P('section', None, 'expert'), may hold values from -6 to 6
- norm_gain: bfloat16 [16, 2048], P('section'), may hold values from 0.099609375 to 1.8984375
- router: bfloat16 [16, 2048, 64], P('section'), may hold values from -0.125 to 0.125
- up_weight: bfloat16 [64, 2048, 1024], P('expert'), may hold values from -0.125 to 0.125
- down_weight: bfloat16 [64, 1024, 2048], P('expert'), may hold values from -0.1875 to 0.1875
Outputs:
- forward_output: bfloat16 [16, 4096, 2048], P('section', 'expert')
- input_gradient: bfloat16 [16, 4096, 2048], P('section', 'expert')
The draws below stay inside these ranges and needn't reach their ends.
Inputs may be any that keep to these rules, and one draw needn't show every extreme that they name: `forward_routes`: in each aligned block of 64 rows (one device's tokens at one section) no expert is named by more than 3 rows, a bound that some block reaches; the 2 entries of a row differ. `backward_routes`: in each aligned block of 64 rows (one device's tokens at one section) no expert is named by more than 3 rows, a bound that some block reaches; the 2 entries of a row differ.
All inputs are finite; a program needn't handle non-finite values.
Results may differ from the reference program's by a relative error of at most 0.0053.
Values may be sent and summed in bfloat16 or wider, within the bound.
A program may use at most 32 MiB of HBM per device.

```python
import math
import jax
import jax.numpy as jnp
import numpy as np
from jax import lax

D = 2048
FF = 1024
EXPERTS = 64
TOP = 2
TOK_DEV = 64
CAP = 3
SECTIONS = 16
BLOCKS = 64
TOKENS = 4096


def block_scale(key, shape, split, low, high):
    loudness = 1.0
    for position, blocks in split:
        steps = jax.random.uniform(jax.random.fold_in(jax.random.fold_in(key, 6), position), (blocks,), jnp.float32, low / len(split), high / len(split))
        loudness = loudness * jnp.repeat(jnp.exp(steps), shape[position] // blocks).reshape((-1,) + (1,) * (len(shape) - 1 - position))
    return loudness


def assign_block(key, own, number, rows, amount, top, reach, slope):
    order = jax.random.permutation(key, amount)
    crowded, usual = portions_of(amount, rows * top, reach, slope, True), portions_of(amount, rows * top, reach, slope, False)
    places = jnp.arange(amount)

    def named(tallies, turn):
        used = int((tallies > 0).sum())
        fixed = max(1, used // 4)
        moved = fixed + (places - fixed + turn * (used - fixed)) % max(1, amount - fixed)
        return jnp.zeros((amount,), jnp.int32).at[order[jnp.where(places < fixed, places, moved)]].set(jnp.asarray(tallies, jnp.int32))

    tallies = jnp.where(number % 4 == 0, named(crowded, number // 4), named(usual, number - number // 4 - 1))
    mixed = jax.random.permutation(jax.random.fold_in(own, 3), amount)
    source_of, sink = mixed[0:amount // 2 * 2:2], mixed[1:amount // 2 * 2:2]
    room = jnp.minimum(tallies[source_of] - 1, reach - tallies[sink]) // 2
    room = jnp.where((source_of == order[0]) | (sink == order[0]) | (tallies[sink] == 0), 0, jnp.maximum(room, 0))
    moved = jax.random.randint(jax.random.fold_in(own, 4), (amount // 2,), 0, 1 << 20) % (room + 1)
    tallies = tallies.at[source_of].add(-moved).at[sink].add(moved)
    labels = jnp.searchsorted(jnp.cumsum(tallies), jnp.arange(rows * top), side="right").astype(jnp.int32)
    grid = labels.reshape(top, rows).T
    grid = grid[jax.random.permutation(jax.random.fold_in(own, 1), rows)]
    turn = jax.random.randint(jax.random.fold_in(own, 2), (rows, 1), 0, top)
    return jnp.take_along_axis(grid, (jnp.arange(top)[None, :] + turn) % top, axis=1)


def portions_of(amount, total, limit, slope, full):
    loads = [(1 << 20) // math.isqrt(rank ** slope) + 1 for rank in range(1, amount + 1)]
    largest = limit if full else min(limit, max(-(-total // amount), total * loads[0] // sum(loads)))
    least = 1 if total - largest >= amount - 1 else 0
    holding, spare = [largest] + [least] * (amount - 1), total - largest - least * (amount - 1)
    while spare > 0:
        free = [i for i in range(1, amount) if holding[i] < largest] or [i for i in range(1, amount) if holding[i] < limit]
        whole, budget = sum([loads[i] for i in free]), spare
        for i in free:
            extra = min(limit - holding[i], max(1, budget * loads[i] // whole), spare)
            holding[i] = holding[i] + extra
            spare = spare - extra
    return np.array(holding)


def normal_values(rng, shape, spread, reach, cuts=(), kind=jnp.bfloat16):
    entries = spread * jax.random.normal(rng, shape, jnp.float32)
    if cuts:
        entries = entries * block_scale(rng, shape, cuts, -0.22, 0.18)
    return jnp.clip(entries, -reach, reach).astype(kind)


def setup_inputs(seed: int = 0) -> dict:
    arg_keys = jax.random.split(jax.random.key(seed), 13)
    forward_sent = normal_values(arg_keys[0], (SECTIONS, TOKENS, D), 1.0, 6.0, ((0, 16), (1, 64)))
    embedded = normal_values(arg_keys[1], (TOKENS, D), 1.0, 6.0, ((0, 64),))
    forward_routes_keys = jax.random.split(jax.random.fold_in(arg_keys[2], 1), SECTIONS * TOKENS // TOK_DEV)
    forward_routes_turns = jax.random.permutation(jax.random.fold_in(arg_keys[2], 3), SECTIONS * TOKENS // TOK_DEV)
    forward_routes = jax.vmap(lambda own, number: assign_block(jax.random.fold_in(arg_keys[2], 2), own, number, TOK_DEV, EXPERTS, TOP, CAP, 2))(forward_routes_keys, forward_routes_turns).reshape((SECTIONS, TOKENS, TOP))
    backward_sent = normal_values(arg_keys[3], (SECTIONS, TOKENS, D), 1.0, 6.0, ((0, 16), (1, 64)))
    loss_gradient = normal_values(arg_keys[4], (TOKENS, D), 1.0, 6.0, ((0, 64),))
    saved_inputs = normal_values(arg_keys[5], (SECTIONS, TOKENS, D), 1.0, 6.0, ((0, 16), (1, 64)))
    backward_routes_keys = jax.random.split(jax.random.fold_in(arg_keys[6], 1), SECTIONS * TOKENS // TOK_DEV)
    backward_routes_turns = jax.random.permutation(jax.random.fold_in(arg_keys[6], 3), SECTIONS * TOKENS // TOK_DEV)
    backward_routes = jax.vmap(lambda own, number: assign_block(jax.random.fold_in(arg_keys[6], 2), own, number, TOK_DEV, EXPERTS, TOP, CAP, 2))(backward_routes_keys, backward_routes_turns).reshape((SECTIONS, TOKENS, TOP))
    pre_activation = normal_values(arg_keys[7], (SECTIONS, BLOCKS, EXPERTS, CAP, FF), 1.0, 6.0, ((0, 16), (2, 64)))
    norm_gain = jnp.clip(1.0 + 0.18 * jax.random.normal(arg_keys[8], (SECTIONS, D), jnp.float32), 0.099609375, 1.8984375).astype(jnp.bfloat16)
    router = normal_values(arg_keys[9], (SECTIONS, D, EXPERTS), D ** -0.5, 0.125, ((0, 16),))
    up_weight = normal_values(arg_keys[10], (EXPERTS, D, FF), D ** -0.5, 0.125, ((0, 64),))
    down_weight = normal_values(arg_keys[11], (EXPERTS, FF, D), FF ** -0.5, 0.1875, ((0, 64),))
    return {"forward_sent": forward_sent, "embedded": embedded, "forward_routes": forward_routes, "backward_sent": backward_sent, "loss_gradient": loss_gradient, "saved_inputs": saved_inputs, "backward_routes": backward_routes, "pre_activation": pre_activation, "norm_gain": norm_gain, "router": router, "up_weight": up_weight, "down_weight": down_weight}


EPS = 1e-06
HIGH = lax.Precision.HIGHEST

def slot_targets(block_routes):
    flattened = block_routes.reshape(-1).astype(jnp.int32)
    onehot = (flattened[:, None] == jnp.arange(EXPERTS, dtype=jnp.int32)[None, :]).astype(jnp.int32)
    before = jnp.cumsum(onehot, axis=0) - onehot
    ranked = lax.optimization_barrier(jnp.sum(before * onehot, axis=1)).astype(jnp.int32)
    return (flattened * CAP + ranked).reshape(block_routes.shape)

def routing(tokens, gain_row, router_mat, routes):
    widened = tokens.astype(jnp.float32)
    inv_rms = lax.rsqrt(lax.optimization_barrier(jnp.mean(widened * widened, axis=-1)) + EPS)
    normed = (widened * inv_rms[:, None] * gain_row.astype(jnp.float32)).astype(jnp.bfloat16)
    logits = jnp.dot(normed.astype(jnp.float32), router_mat.astype(jnp.float32), precision=HIGH)
    chosen = jnp.take_along_axis(logits, routes, axis=1)
    exponent = jnp.exp(chosen)
    shares = exponent / lax.optimization_barrier(jnp.sum(exponent, axis=1, keepdims=True))
    rounded = lax.optimization_barrier(shares.astype(jnp.bfloat16)).astype(jnp.float32)
    targets = jax.vmap(slot_targets)(routes.reshape(BLOCKS, TOK_DEV, TOP))
    slot_table = (targets[..., None] == jnp.arange(EXPERTS * CAP, dtype=jnp.int32)).astype(jnp.float32)
    placing = lax.optimization_barrier(jnp.sum(slot_table, axis=2))
    mixing = lax.optimization_barrier(jnp.sum(slot_table * rounded.reshape(BLOCKS, TOK_DEV, TOP)[..., None], axis=2))
    return (widened, inv_rms, normed, shares, slot_table, placing, mixing)

def dispatch(placing, data):
    blocked = data.reshape(BLOCKS, TOK_DEV, D).astype(jnp.float32)
    sent_rows = jnp.einsum('jts,jtd->jsd', placing, blocked, precision=HIGH).astype(jnp.bfloat16)
    return sent_rows.reshape(BLOCKS, EXPERTS, CAP, D).transpose(1, 0, 2, 3)

def forward_section(tokens, routes, gain_row, router_mat, up_weight, down_weight):
    widened, inv_rms, normed, shares, slot_table, placing, mixing = routing(tokens, gain_row, router_mat, routes)
    per_expert = dispatch(placing, normed)

    def expert(operands):
        block_rows, up_mat, down_mat = operands
        flattened = block_rows.reshape(-1, D).astype(jnp.float32)
        pre_act = jnp.dot(flattened, up_mat.astype(jnp.float32), precision=HIGH)
        hidden = lax.optimization_barrier(jax.nn.silu(pre_act).astype(jnp.bfloat16)).astype(jnp.float32)
        result = jnp.dot(hidden, down_mat.astype(jnp.float32), precision=HIGH).astype(jnp.bfloat16)
        return result.reshape(BLOCKS, CAP, D)
    outputs = lax.map(expert, (per_expert, up_weight, down_weight))
    outputs = outputs.transpose(1, 0, 2, 3).reshape(BLOCKS, EXPERTS * CAP, D).astype(jnp.float32)
    expert_sum = jnp.einsum('jts,jsd->jtd', mixing, outputs, precision=HIGH).reshape(TOKENS, D)
    return (widened + expert_sum).astype(jnp.bfloat16)

def backward_section(tokens, upstream, routes, saved_pre, gain_row, router_mat, up_weight, down_weight):
    widened, inv_rms, normed, shares, slot_table, placing, mixing = routing(tokens, gain_row, router_mat, routes)
    per_expert = dispatch(placing, upstream)
    saved_view = saved_pre.transpose(1, 0, 2, 3)

    def expert(operands):
        block_rows, saved_block, up_mat, down_mat = operands
        grad_rows = block_rows.reshape(-1, D).astype(jnp.float32)
        pre_act = saved_block.reshape(-1, FF).astype(jnp.float32)
        hidden_grad = jnp.dot(grad_rows, down_mat.astype(jnp.float32).T, precision=HIGH)
        hidden_rounded = lax.optimization_barrier(jax.nn.silu(pre_act).astype(jnp.bfloat16)).astype(jnp.float32)
        inner_sums = lax.optimization_barrier(jnp.sum(hidden_grad * hidden_rounded, axis=-1)).astype(jnp.bfloat16)
        sigmoid_pre = jax.nn.sigmoid(pre_act)
        pre_grad = hidden_grad * sigmoid_pre * (1.0 + pre_act * (1.0 - sigmoid_pre))
        pre_grad = lax.optimization_barrier(pre_grad.astype(jnp.bfloat16)).astype(jnp.float32)
        input_rows = jnp.dot(pre_grad, up_mat.astype(jnp.float32).T, precision=HIGH).astype(jnp.bfloat16)
        return (input_rows.reshape(BLOCKS, CAP, D), inner_sums.reshape(BLOCKS, CAP))
    input_rows, inner_sums = lax.map(expert, (per_expert, saved_view, up_weight, down_weight))
    input_rows = input_rows.transpose(1, 0, 2, 3).reshape(BLOCKS, EXPERTS * CAP, D).astype(jnp.float32)
    inner_sums = inner_sums.transpose(1, 0, 2).reshape(BLOCKS, EXPERTS * CAP).astype(jnp.float32)
    normed_grad = jnp.einsum('jts,jsd->jtd', mixing, input_rows, precision=HIGH).reshape(TOKENS, D)
    route_sums = jnp.einsum('jtks,js->jtk', slot_table, inner_sums, precision=HIGH).reshape(TOKENS, TOP)
    chosen_grad = shares * (route_sums - lax.optimization_barrier(jnp.sum(shares * route_sums, axis=1, keepdims=True)))
    route_hits = (routes[..., None] == jnp.arange(EXPERTS, dtype=jnp.int32)).astype(jnp.float32)
    logit_grad = jnp.einsum('tk,tke->te', chosen_grad, route_hits, precision=HIGH)
    normed_grad = normed_grad + jnp.dot(logit_grad, router_mat.astype(jnp.float32).T, precision=HIGH)
    gained_grad = normed_grad * gain_row.astype(jnp.float32)
    input_grad = inv_rms[:, None] * gained_grad - widened * (inv_rms ** 3)[:, None] * lax.optimization_barrier(jnp.mean(widened * gained_grad, axis=-1, keepdims=True))
    return (upstream.astype(jnp.float32) + input_grad).astype(jnp.bfloat16)

def reference(forward_sent, embedded, forward_routes, backward_sent, loss_gradient, saved_inputs, backward_routes, pre_activation, norm_gain, router, up_weight, down_weight):
    section_input = jnp.concatenate([embedded[None], forward_sent[:-1]], axis=0)
    upstream = jnp.concatenate([backward_sent[1:], loss_gradient[None]], axis=0)

    def run_forward(operands):
        tokens, routes, gain_row, router_mat = operands
        return forward_section(tokens, routes, gain_row, router_mat, up_weight, down_weight)

    def run_backward(operands):
        tokens, grads, routes, saved_pre, gain_row, router_mat = operands
        return backward_section(tokens, grads, routes, saved_pre, gain_row, router_mat, up_weight, down_weight)
    forward_output = lax.map(run_forward, (section_input, forward_routes, norm_gain, router))
    input_gradient = lax.map(run_backward, (saved_inputs, upstream, backward_routes, pre_activation, norm_gain, router))
    return (forward_output, input_gradient)
```

```python
import functools

import jax
import jax.numpy as jnp
from jax import lax
from jax.experimental import pallas as pl
from jax.experimental.pallas import tpu as pltpu
from jax.sharding import PartitionSpec as P

EPS = 1e-06
HIGH = lax.Precision.HIGHEST
LANE = 128


def from_behind(block, axis, distance):
    devices = range(lax.axis_size(axis))
    route = [(i - distance, i) for i in devices if i - distance in devices]
    return lax.ppermute(block, axis, route)


def slot_targets(routes, experts, capacity):
    flattened = routes.reshape(-1)
    onehot = (flattened[:, None] == jnp.arange(experts, dtype=jnp.int32)[None, :]).astype(jnp.int32)
    before = jnp.cumsum(onehot, axis=0) - onehot
    ranked = jnp.sum(before * onehot, axis=1)
    return (flattened * capacity + ranked).reshape(routes.shape)


def prepare_routes(tokens, gain_row, router_mat, routes, experts, capacity):
    widened = tokens.astype(jnp.float32)
    inv_rms = lax.rsqrt(jnp.mean(widened * widened, axis=-1) + EPS)
    normed = (widened * inv_rms[:, None] * gain_row.astype(jnp.float32)).astype(jnp.bfloat16)
    logits = jnp.dot(normed, router_mat, preferred_element_type=jnp.float32)
    chosen = jnp.take_along_axis(logits, routes, axis=1)
    exponent = jnp.exp(chosen)
    shares = exponent / jnp.sum(exponent, axis=1, keepdims=True)
    rounded = lax.optimization_barrier(shares.astype(jnp.bfloat16)).astype(jnp.float32)
    targets = slot_targets(routes, experts, capacity)
    slot_table = (targets[..., None] == jnp.arange(experts * capacity, dtype=jnp.int32)).astype(
        jnp.float32
    )
    placing = jnp.sum(slot_table, axis=1).astype(jnp.bfloat16)
    mixing = jnp.sum(slot_table * rounded[..., None], axis=1).astype(jnp.bfloat16)
    return (widened, inv_rms, normed, shares, slot_table, placing, mixing)


def relay_kernel(
    devices,
    capacity,
    send_f,
    send_b,
    pre_hbm,
    up_hbm,
    down_hbm,
    out_f,
    out_b,
    out_s,
    pre,
    up,
    down,
    got_f,
    got_b,
    ret_f,
    ret_b,
    ret_s,
    wide,
    mid,
    load_sem,
    send_sem,
    recv_sem,
    small_send,
    small_recv,
):
    me = lax.axis_index("expert")
    chips = devices // 2
    spot, core = me // 2, lax.rem(me, 2)
    hidden_size, width = down.shape
    rows = devices * capacity
    sub = width // LANE
    entry = capacity * sub
    group = 32
    tile = 256

    loads = [
        pltpu.make_async_copy(pre_hbm, pre, load_sem.at[0]),
        pltpu.make_async_copy(down_hbm, down, load_sem.at[1]),
        pltpu.make_async_copy(up_hbm, up, load_sem.at[2]),
    ]
    for load in loads:
        load.start()

    barrier = pltpu.get_barrier_semaphore()
    for step in range(1, devices):
        pl.semaphore_signal(
            barrier, 1, device_id={"expert": lax.rem(me + step, devices)}
        )
    pl.semaphore_wait(barrier, devices - 1)

    peers = []
    for distance in range(chips // 2, -1, -1):
        ways = (1,) if distance in (0, chips // 2) else (1, -1)
        for way in ways:
            for other in (0, 1):
                if distance or other:
                    place = lax.rem(spot + way * distance + chips, chips)
                    peers.append(place * 2 + lax.rem(core + other, 2))

    def part(ref, device):
        return ref.at[pl.ds(pl.multiple_of(device * entry, entry), entry), :]

    def exchange(stage, source, target):
        copies = []
        for number, peer in enumerate(peers):
            copy = pltpu.make_async_remote_copy(
                src_ref=part(source, peer),
                dst_ref=part(target, me),
                send_sem=send_sem.at[stage, number],
                recv_sem=recv_sem.at[stage, number],
                device_id={"expert": peer},
            )
            copy.start()
            copies.append(copy)
        own = pl.ds(pl.multiple_of(me * entry, entry), entry)
        target[own, :] = source[own, :]
        return copies

    def arrive(copies):
        for copy in copies:
            copy.wait_recv()

    def iota(shape, axis):
        return lax.broadcasted_iota(jnp.int32, shape, axis)

    def onehot(condition):
        return jnp.where(condition, 1.0, 0.0).astype(jnp.bfloat16)

    side = group * sub
    to_wide = onehot(
        iota((side, side), 1)
        == lax.rem(iota((side, side), 0), group) * sub + iota((side, side), 0) // group
    )
    to_lanes = onehot(
        iota((side, side), 0)
        == lax.rem(iota((side, side), 1), group) * sub + iota((side, side), 1) // group
    )

    def widen(source):
        @pl.loop(0, rows // group)
        def _(number):
            block = source[pl.ds(pl.multiple_of(number * side, side), side), :]
            moved = jnp.dot(to_wide, block, preferred_element_type=jnp.float32).astype(
                jnp.bfloat16
            )
            here = pl.ds(pl.multiple_of(number * group, group), group)
            for k in range(sub):
                wide[here, k * LANE : (k + 1) * LANE] = moved[
                    k * group : (k + 1) * group, :
                ]

    def narrow(target):
        @pl.loop(0, rows // group)
        def _(number):
            here = pl.ds(pl.multiple_of(number * group, group), group)
            block = jnp.concatenate(
                [wide[here, k * LANE : (k + 1) * LANE] for k in range(sub)], axis=0
            )
            target[pl.ds(pl.multiple_of(number * side, side), side), :] = jnp.dot(
                to_lanes, block, preferred_element_type=jnp.float32
            ).astype(jnp.bfloat16)

    def columns(number):
        return pl.ds(pl.multiple_of(number * tile, tile), tile)

    def transposed(left, right):
        return lax.dot_general(
            left, right, (((1,), (1,)), ((), ())), preferred_element_type=jnp.float32
        )

    sent_b = exchange(0, send_b, got_b)
    sent_f = exchange(1, send_f, got_f)

    for load in loads:
        load.wait()
    arrive(sent_b)
    widen(got_b)
    pick = onehot(
        iota((rows, rows), 1)
        == lax.rem(iota((rows, rows), 0), capacity) * devices
        + iota((rows, rows), 0) // capacity
    )

    def back_tile(number, inner):
        grad = transposed(wide[...], down[columns(number), :])
        value = jnp.dot(
            pick, pre[:, columns(number)], preferred_element_type=jnp.float32
        )
        gate = jax.nn.sigmoid(value)
        rounded = (value * gate).astype(jnp.bfloat16).astype(jnp.float32)
        mid[:, columns(number)] = (
            grad * gate * (1.0 + value * (1.0 - gate))
        ).astype(jnp.bfloat16)
        return inner + jnp.sum(grad * rounded, axis=1, keepdims=True)

    inner = lax.fori_loop(
        0, hidden_size // tile, back_tile, jnp.zeros((rows, 1), jnp.float32)
    )
    spread = jnp.where(
        iota((rows, LANE), 1) == lax.rem(iota((rows, LANE), 0), capacity), inner, 0.0
    ).astype(jnp.bfloat16)
    gather = onehot(
        iota((devices, rows), 0) == iota((devices, rows), 1) // capacity
    )
    sums = jnp.dot(gather, spread, preferred_element_type=jnp.float32)
    for number in range(devices):
        ret_s[number] = sums[number : number + 1, :]

    @pl.loop(0, width // tile)
    def _(number):
        wide[:, columns(number)] = transposed(
            mid[...], up[columns(number), :]
        ).astype(jnp.bfloat16)

    narrow(ret_b)
    small = []
    for number, peer in enumerate(peers):
        copy = pltpu.make_async_remote_copy(
            src_ref=ret_s.at[peer],
            dst_ref=out_s.at[me],
            send_sem=small_send.at[number],
            recv_sem=small_recv.at[number],
            device_id={"expert": peer},
        )
        copy.start()
        small.append(copy)
    out_s[me] = ret_s[me]
    back_b = exchange(2, ret_b, out_b)

    arrive(sent_f)
    widen(got_f)

    @pl.loop(0, hidden_size // tile)
    def _(number):
        value = jnp.dot(
            wide[...], up[:, columns(number)], preferred_element_type=jnp.float32
        )
        mid[:, columns(number)] = jax.nn.silu(value).astype(jnp.bfloat16)

    @pl.loop(0, width // tile)
    def _(number):
        wide[:, columns(number)] = jnp.dot(
            mid[...], down[:, columns(number)], preferred_element_type=jnp.float32
        ).astype(jnp.bfloat16)

    narrow(ret_f)
    back_f = exchange(3, ret_f, out_f)
    arrive(small)
    arrive(back_b)
    arrive(back_f)
    for copy in sent_b + sent_f + small + back_b + back_f:
        copy.wait_send()


def relay(send_f, send_b, pre, up_mat, down_mat, devices, capacity):
    lanes = send_f.shape
    hidden_size, width = down_mat.shape
    rows = devices * capacity
    vmem = pl.BlockSpec(memory_space=pltpu.VMEM)
    anywhere = pl.BlockSpec(memory_space=pl.ANY)
    row_type = jax.ShapeDtypeStruct(lanes, jnp.bfloat16)
    return pl.pallas_call(
        functools.partial(relay_kernel, devices, capacity),
        out_shape=(
            row_type,
            row_type,
            jax.ShapeDtypeStruct((devices, 1, LANE), jnp.float32),
        ),
        in_specs=[vmem, vmem, anywhere, anywhere, anywhere],
        out_specs=(vmem, vmem, vmem),
        scratch_shapes=[
            pltpu.VMEM(pre.shape, jnp.bfloat16),
            pltpu.VMEM(up_mat.shape, jnp.bfloat16),
            pltpu.VMEM(down_mat.shape, jnp.bfloat16),
            pltpu.VMEM(lanes, jnp.bfloat16),
            pltpu.VMEM(lanes, jnp.bfloat16),
            pltpu.VMEM(lanes, jnp.bfloat16),
            pltpu.VMEM(lanes, jnp.bfloat16),
            pltpu.VMEM((devices, 1, LANE), jnp.float32),
            pltpu.VMEM((rows, width), jnp.bfloat16),
            pltpu.VMEM((rows, hidden_size), jnp.bfloat16),
            pltpu.SemaphoreType.DMA((3,)),
            pltpu.SemaphoreType.DMA((4, devices)),
            pltpu.SemaphoreType.DMA((4, devices)),
            pltpu.SemaphoreType.DMA((devices,)),
            pltpu.SemaphoreType.DMA((devices,)),
        ],
        compiler_params=pltpu.CompilerParams(
            collective_id=0, has_side_effects=True, vmem_limit_bytes=48 << 20
        ),
    )(send_f, send_b, pre, up_mat, down_mat)


def on_device(
    forward_sent,
    embedded,
    forward_routes,
    backward_sent,
    loss_gradient,
    saved_inputs,
    backward_routes,
    pre_activation,
    norm_gain,
    router,
    up_weight,
    down_weight,
):
    section_index = lax.axis_index("section")
    final_section = lax.axis_size("section") - 1
    sources = lax.axis_size("expert")
    experts = router.shape[2]
    capacity = pre_activation.shape[3]
    width = up_weight.shape[1]
    slots = experts * capacity
    gain_row = norm_gain[0]
    router_mat = router[0]
    arrived = from_behind(forward_sent[0], "section", 1)
    tokens = jnp.where(section_index == 0, embedded, arrived)
    returned_grad = from_behind(backward_sent[0], "section", -1)
    upstream = jnp.where(section_index == final_section, loss_gradient, returned_grad)
    widened, inv_rms, normed, shares, slot_table, placing, mixing = prepare_routes(
        tokens, gain_row, router_mat, forward_routes[0], experts, capacity
    )
    saved_wide, saved_rms, saved_normed, saved_shares, saved_table, saved_placing, saved_mixing = (
        prepare_routes(saved_inputs[0], gain_row, router_mat, backward_routes[0], experts, capacity)
    )
    send_forward = jnp.einsum(
        "ts,td->sd", placing, normed, preferred_element_type=jnp.float32
    ).astype(jnp.bfloat16)
    send_backward = jnp.einsum(
        "ts,td->sd", saved_placing, upstream, preferred_element_type=jnp.float32
    ).astype(jnp.bfloat16)
    saved_pre = pre_activation[0, :, 0].transpose(1, 0, 2).reshape(slots, -1)
    back_forward, back_rows, back_sums = relay(
        send_forward.reshape(-1, LANE),
        send_backward.reshape(-1, LANE),
        saved_pre,
        up_weight[0],
        down_weight[0],
        sources,
        capacity,
    )
    back_sums = back_sums[:, 0, :capacity]
    expert_sum = jnp.dot(
        mixing, back_forward.reshape(slots, width), preferred_element_type=jnp.float32
    )
    forward_output = (widened + expert_sum).astype(jnp.bfloat16)
    normed_grad = jnp.dot(
        saved_mixing, back_rows.reshape(slots, width), preferred_element_type=jnp.float32
    )
    route_sums = jnp.einsum(
        "tks,s->tk", saved_table, back_sums.reshape(slots).astype(jnp.float32), precision=HIGH
    )
    chosen_grad = saved_shares * (
        route_sums - jnp.sum(saved_shares * route_sums, axis=1, keepdims=True)
    )
    route_hits = (backward_routes[0][..., None] == jnp.arange(experts, dtype=jnp.int32)).astype(
        jnp.float32
    )
    logit_grad = jnp.einsum("tk,tke->te", chosen_grad, route_hits, precision=HIGH)
    normed_grad = normed_grad + jnp.dot(
        logit_grad, router_mat.astype(jnp.float32).T, precision=HIGH
    )
    gained_grad = normed_grad * gain_row.astype(jnp.float32)
    input_grad = saved_rms[:, None] * gained_grad - saved_wide * (saved_rms**3)[
        :, None
    ] * jnp.mean(saved_wide * gained_grad, axis=-1, keepdims=True)
    input_gradient = (upstream.astype(jnp.float32) + input_grad).astype(jnp.bfloat16)
    return (forward_output[None], input_gradient[None])


def solution(mesh):
    return jax.shard_map(
        on_device,
        mesh=mesh,
        in_specs=(
            P("section", "expert", None),
            P("expert", None),
            P("section", "expert", None),
            P("section", "expert", None),
            P("expert", None),
            P("section", "expert", None),
            P("section", "expert", None),
            P("section", None, "expert", None, None),
            P("section", None),
            P("section", None, None),
            P("expert", None, None),
            P("expert", None, None),
        ),
        out_specs=(P("section", "expert", None), P("section", "expert", None)),
        check_vma=False,
    )
```

```python
import functools

import jax
import jax.numpy as jnp
from jax import lax
from jax.experimental import pallas as pl
from jax.experimental.pallas import tpu as pltpu
from jax.sharding import PartitionSpec as P

EPS = 1e-06
HIGH = lax.Precision.HIGHEST
LANE = 128
TILE = 256
GROUP = 32


def iota(shape, axis):
    return lax.broadcasted_iota(jnp.int32, shape, axis)


def onehot(condition):
    return jnp.where(condition, 1.0, 0.0).astype(jnp.bfloat16)


def dot(left, right, precision=None):
    return jnp.dot(
        left, right, preferred_element_type=jnp.float32, precision=precision
    )


def dot_transposed(left, right, precision=None):
    return lax.dot_general(
        left,
        right,
        (((1,), (1,)), ((), ())),
        preferred_element_type=jnp.float32,
        precision=precision,
    )


def columns(number):
    return pl.ds(pl.multiple_of(number * TILE, TILE), TILE)


def relay_kernel(
    sizes,
    forward_hbm,
    backward_hbm,
    routes_b_hbm,
    loss_hbm,
    routes_f_hbm,
    embedded_hbm,
    gain_hbm,
    router_hbm,
    down_hbm,
    pre_hbm,
    up_hbm,
    saved_hbm,
    out_f,
    out_b,
    routes_b,
    loss,
    routes_f,
    embedded,
    gain,
    router,
    down,
    pre,
    up,
    saved,
    arrived,
    returned,
    tokens,
    upstream,
    normed,
    mixing,
    gained,
    send_f,
    send_b,
    got_f,
    got_b,
    ret_f,
    ret_b,
    back_f,
    back_b,
    ret_s,
    back_s,
    wide,
    mid,
    load_sem,
    send_sem,
    recv_sem,
    pass_send,
    pass_recv,
):
    devices, sections, experts, capacity = sizes
    section = lax.axis_index("section")
    me = lax.axis_index("expert")
    chips = devices // 2
    spot, core = me // 2, lax.rem(me, 2)
    hidden_size, width = down.shape
    count = tokens.shape[0]
    rows = experts * capacity
    sub = width // LANE
    entry = capacity * sub

    barrier = pltpu.get_barrier_semaphore()
    ahead = {"section": lax.rem(section + 1, sections)}
    behind = {"section": lax.rem(section + sections - 1, sections)}
    pl.semaphore_signal(barrier, 1, device_id=ahead)
    pl.semaphore_signal(barrier, 1, device_id=behind)

    @pl.loop(1, devices)
    def _(step):
        pl.semaphore_signal(
            barrier, 1, device_id={"expert": lax.rem(me + step, devices)}
        )

    pairs = (
        (routes_b_hbm, routes_b),
        (loss_hbm, loss),
        (routes_f_hbm, routes_f),
        (embedded_hbm, embedded),
        (gain_hbm, gain),
        (router_hbm, router),
        (down_hbm, down),
        (pre_hbm, pre),
        (up_hbm, up),
        (saved_hbm, saved),
    )
    loads = [
        pltpu.make_async_copy(source, target, load_sem.at[number])
        for number, (source, target) in enumerate(pairs)
    ]
    for load in loads:
        load.start()

    def peer_of(number):
        place = number + 2
        distance = chips // 2 - place // 4
        way = 2 * lax.rem(place // 2, 2) - 1
        spot_there = lax.rem(spot + way * distance + chips, chips)
        return spot_there * 2 + lax.rem(core + number, 2)

    def part(ref, device):
        return ref.at[pl.ds(pl.multiple_of(device * entry, entry), entry), :]

    def copy_of(stage, number, peer, source, target):
        if stage < 4:
            here, there = part(source, peer), part(target, me)
        else:
            here, there = source.at[peer], target.at[me]
        return pltpu.make_async_remote_copy(
            src_ref=here,
            dst_ref=there,
            send_sem=send_sem.at[stage, number],
            recv_sem=recv_sem.at[stage, number],
            device_id={"expert": peer},
        )

    partner = spot * 2 + 1 - core

    def for_peers(act):
        @pl.loop(0, devices - 2)
        def _(number):
            act(number, peer_of(number))

        act(devices - 2, partner)

    def exchange(stage, source, target):
        for_peers(
            lambda number, peer: copy_of(stage, number, peer, source, target).start()
        )
        if stage < 4:
            own = pl.ds(pl.multiple_of(me * entry, entry), entry)
            target[own, :] = source[own, :]
        else:
            target[me] = source[me]

    def arrive(stage, source, target):
        for_peers(
            lambda number, peer: copy_of(
                stage, number, peer, source, target
            ).wait_recv()
        )

    def leave(stage, source, target):
        for_peers(
            lambda number, peer: copy_of(
                stage, number, peer, source, target
            ).wait_send()
        )

    side = GROUP * sub
    to_wide = onehot(
        iota((side, side), 1)
        == lax.rem(iota((side, side), 0), GROUP) * sub + iota((side, side), 0) // GROUP
    )
    to_lanes = onehot(
        iota((side, side), 0)
        == lax.rem(iota((side, side), 1), GROUP) * sub + iota((side, side), 1) // GROUP
    )

    def widen(source):
        @pl.loop(0, rows // GROUP)
        def _(number):
            block = source[pl.ds(pl.multiple_of(number * side, side), side), :]
            moved = dot(to_wide, block).astype(jnp.bfloat16)
            here = pl.ds(pl.multiple_of(number * GROUP, GROUP), GROUP)
            for k in range(sub):
                wide[here, k * LANE : (k + 1) * LANE] = moved[
                    k * GROUP : (k + 1) * GROUP, :
                ]

    def narrow(target):
        @pl.loop(0, rows // GROUP)
        def _(number):
            here = pl.ds(pl.multiple_of(number * GROUP, GROUP), GROUP)
            block = jnp.concatenate(
                [wide[here, k * LANE : (k + 1) * LANE] for k in range(sub)], axis=0
            )
            target[pl.ds(pl.multiple_of(number * side, side), side), :] = dot(
                to_lanes, block
            ).astype(jnp.bfloat16)

    earlier = onehot(iota((count, count), 0) < iota((count, count), 1))
    identity = onehot(iota((count, count), 0) == iota((count, count), 1))

    def follow(routes):
        named = [routes[k : k + 1, :] for k in range(routes.shape[0])]
        hits = [iota((experts, count), 0) == name for name in named]
        chosen = onehot(hits[0])
        for hit in hits[1:]:
            chosen = chosen + onehot(hit)
        before = dot(chosen, earlier)
        ranks = [
            jnp.sum(jnp.where(hit, before, 0.0), axis=0, keepdims=True) for hit in hits
        ]
        slot_number = iota((rows, count), 0).astype(jnp.float32)
        places = [
            slot_number == name.astype(jnp.float32) * capacity + rank
            for name, rank in zip(named, ranks)
        ]
        return hits, ranks, places

    def dispatch(places, source, target):
        placing = onehot(places[0])
        for place in places[1:]:
            placing = placing + onehot(place)

        @pl.loop(0, width // TILE)
        def _(number):
            wide[:, columns(number)] = dot(
                placing, source[:, columns(number)]
            ).astype(jnp.bfloat16)

        narrow(target)

    def normalise(source):
        def add(number, total):
            value = source[:, columns(number)].astype(jnp.float32)
            return total + jnp.sum(value * value, axis=1, keepdims=True)

        total = lax.fori_loop(
            0, width // TILE, add, jnp.zeros((count, 1), jnp.float32)
        )
        inv_rms = lax.rsqrt(total / width + EPS)

        @pl.loop(0, width // TILE)
        def _(number):
            value = source[:, columns(number)].astype(jnp.float32)
            scale = gain[:, columns(number)].astype(jnp.float32)
            normed[:, columns(number)] = (value * inv_rms * scale).astype(jnp.bfloat16)

        return inv_rms

    def share(hits, places):
        logits = dot_transposed(router[...], normed[...])
        powers = [
            jnp.exp(jnp.sum(jnp.where(hit, logits, 0.0), axis=0, keepdims=True))
            for hit in hits
        ]
        whole = powers[0]
        for power in powers[1:]:
            whole = whole + power
        shares = [power / whole for power in powers]
        mixed = jnp.zeros((rows, count), jnp.float32)
        for portion, place in zip(shares, places):
            rounded = portion.astype(jnp.bfloat16).astype(jnp.float32)
            mixed = mixed + jnp.where(place, rounded, 0.0)
        mixed = dot_transposed(identity, mixed.astype(jnp.bfloat16))
        return shares, mixed.astype(jnp.bfloat16)

    for load in loads[:2]:
        load.wait()
    hits_b, ranks_b, places_b = follow(routes_b)
    pl.semaphore_wait(barrier, devices + 1)
    pass_back = pltpu.make_async_remote_copy(
        src_ref=backward_hbm,
        dst_ref=returned,
        send_sem=pass_send.at[0],
        recv_sem=pass_recv.at[0],
        device_id=behind,
    )
    pass_on = pltpu.make_async_remote_copy(
        src_ref=forward_hbm,
        dst_ref=arrived,
        send_sem=pass_send.at[1],
        recv_sem=pass_recv.at[1],
        device_id=ahead,
    )
    pass_back.start()
    pass_on.start()
    pass_back.wait_recv()
    upstream[...] = jnp.where(section == sections - 1, loss[...], returned[...])
    dispatch(places_b, upstream, send_b)
    exchange(0, send_b, got_b)

    for load in loads[2:6]:
        load.wait()
    hits_f, _, places_f = follow(routes_f)
    pass_on.wait_recv()
    tokens[...] = jnp.where(section == 0, embedded[...], arrived[...])
    normalise(tokens)
    dispatch(places_f, normed, send_f)
    exchange(1, send_f, got_f)
    mixing[...] = share(hits_f, places_f)[1]

    for load in loads[6:]:
        load.wait()
    arrive(0, send_b, got_b)
    widen(got_b)
    pick = onehot(
        iota((rows, rows), 1)
        == lax.rem(iota((rows, rows), 0), capacity) * devices
        + iota((rows, rows), 0) // capacity
    )

    def back_tile(number, inner):
        grad = dot_transposed(wide[...], down[columns(number), :])
        value = dot(pick, pre[:, columns(number)])
        gate = jax.nn.sigmoid(value)
        rounded = (value * gate).astype(jnp.bfloat16).astype(jnp.float32)
        mid[:, columns(number)] = (
            grad * gate * (1.0 + value * (1.0 - gate))
        ).astype(jnp.bfloat16)
        return inner + jnp.sum(grad * rounded, axis=1, keepdims=True)

    inner = lax.fori_loop(
        0, hidden_size // TILE, back_tile, jnp.zeros((rows, 1), jnp.float32)
    )
    spread = jnp.where(
        iota((rows, LANE), 1) == lax.rem(iota((rows, LANE), 0), capacity), inner, 0.0
    ).astype(jnp.bfloat16)
    gather = onehot(iota((devices, rows), 0) == iota((devices, rows), 1) // capacity)
    sums = dot(gather, spread)
    for number in range(devices):
        ret_s[number] = sums[number : number + 1, :]

    @pl.loop(0, width // TILE)
    def _(number):
        wide[:, columns(number)] = dot_transposed(
            mid[...], up[columns(number), :]
        ).astype(jnp.bfloat16)

    narrow(ret_b)
    exchange(4, ret_s, back_s)
    exchange(2, ret_b, back_b)

    arrive(1, send_f, got_f)
    widen(got_f)

    @pl.loop(0, hidden_size // TILE)
    def _(number):
        value = dot(wide[...], up[:, columns(number)])
        mid[:, columns(number)] = jax.nn.silu(value).astype(jnp.bfloat16)

    @pl.loop(0, width // TILE)
    def _(number):
        wide[:, columns(number)] = dot(mid[...], down[:, columns(number)]).astype(
            jnp.bfloat16
        )

    narrow(ret_f)
    exchange(3, ret_f, back_f)

    inv_rms = normalise(saved)
    shares_b, mixed_b = share(hits_b, places_b)
    arrive(4, ret_s, back_s)
    table = jnp.concatenate([back_s[number] for number in range(experts)], axis=0)
    totals = []
    for hit, rank in zip(hits_b, ranks_b):
        total = jnp.zeros((1, count), jnp.float32)
        for slot in range(capacity):
            named = jnp.sum(
                jnp.where(hit, table[:, slot : slot + 1], 0.0), axis=0, keepdims=True
            )
            total = total + jnp.where(rank == slot, named, 0.0)
        totals.append(total)
    whole = shares_b[0] * totals[0]
    for portion, total in zip(shares_b[1:], totals[1:]):
        whole = whole + portion * total
    logit_grad = jnp.zeros((experts, count), jnp.float32)
    for hit, portion, total in zip(hits_b, shares_b, totals):
        logit_grad = logit_grad + jnp.where(hit, portion * (total - whole), 0.0)
    logit_grad = dot_transposed(identity.astype(jnp.float32), logit_grad, HIGH)
    arrive(2, ret_b, back_b)
    widen(back_b)

    def grad_tile(number, total):
        grad = dot(mixed_b, wide[:, columns(number)]) + dot(
            logit_grad, router[:, columns(number)].astype(jnp.float32), HIGH
        )
        grad = grad * gain[:, columns(number)].astype(jnp.float32)
        gained[:, columns(number)] = grad
        value = saved[:, columns(number)].astype(jnp.float32)
        return total + jnp.sum(value * grad, axis=1, keepdims=True)

    total = lax.fori_loop(
        0, width // TILE, grad_tile, jnp.zeros((count, 1), jnp.float32)
    )
    along = inv_rms * inv_rms * inv_rms * (total / width)

    @pl.loop(0, width // TILE)
    def _(number):
        value = saved[:, columns(number)].astype(jnp.float32)
        grad = inv_rms * gained[:, columns(number)] - value * along
        out_b[:, columns(number)] = (
            upstream[:, columns(number)].astype(jnp.float32) + grad
        ).astype(jnp.bfloat16)

    arrive(3, ret_f, back_f)
    widen(back_f)

    @pl.loop(0, width // TILE)
    def _(number):
        value = tokens[:, columns(number)].astype(jnp.float32)
        out_f[:, columns(number)] = (
            value + dot(mixing[...], wide[:, columns(number)])
        ).astype(jnp.bfloat16)

    pass_back.wait_send()
    pass_on.wait_send()
    leave(0, send_b, got_b)
    leave(1, send_f, got_f)
    leave(2, ret_b, back_b)
    leave(3, ret_f, back_f)
    leave(4, ret_s, back_s)


def on_device(
    forward_sent,
    embedded,
    forward_routes,
    backward_sent,
    loss_gradient,
    saved_inputs,
    backward_routes,
    pre_activation,
    norm_gain,
    router,
    up_weight,
    down_weight,
):
    devices = lax.axis_size("expert")
    sections = lax.axis_size("section")
    experts = router.shape[2]
    capacity = pre_activation.shape[3]
    count, width = embedded.shape
    hidden_size = up_weight.shape[2]
    slots = experts * capacity
    saved_pre = pre_activation[0, :, 0].transpose(1, 0, 2).reshape(slots, hidden_size)
    vmem = pl.BlockSpec(memory_space=pltpu.VMEM)
    hbm = pl.BlockSpec(memory_space=pltpu.HBM)
    block = jax.ShapeDtypeStruct((count, width), jnp.bfloat16)
    held = pltpu.VMEM((count, width), jnp.bfloat16)
    lanes = pltpu.VMEM((slots * width // LANE, LANE), jnp.bfloat16)
    small = pltpu.VMEM((devices, 1, LANE), jnp.float32)
    forward_output, input_gradient = pl.pallas_call(
        functools.partial(relay_kernel, (devices, sections, experts, capacity)),
        out_shape=(block, block),
        in_specs=[hbm] * 12,
        out_specs=(vmem, vmem),
        scratch_shapes=[
            pltpu.VMEM(forward_routes.shape[:0:-1], jnp.int32),
            held,
            pltpu.VMEM(forward_routes.shape[:0:-1], jnp.int32),
            held,
            pltpu.VMEM((1, width), jnp.bfloat16),
            pltpu.VMEM((experts, width), jnp.bfloat16),
            pltpu.VMEM((hidden_size, width), jnp.bfloat16),
            pltpu.VMEM((slots, hidden_size), jnp.bfloat16),
            pltpu.VMEM((width, hidden_size), jnp.bfloat16),
            held,
            held,
            held,
            held,
            held,
            held,
            pltpu.VMEM((count, slots), jnp.bfloat16),
            pltpu.VMEM((count, width), jnp.float32),
            *[lanes] * 8,
            small,
            small,
            pltpu.VMEM((slots, width), jnp.bfloat16),
            pltpu.VMEM((slots, hidden_size), jnp.bfloat16),
            pltpu.SemaphoreType.DMA((10,)),
            pltpu.SemaphoreType.DMA((5, devices)),
            pltpu.SemaphoreType.DMA((5, devices)),
            pltpu.SemaphoreType.DMA((2,)),
            pltpu.SemaphoreType.DMA((2,)),
        ],
        compiler_params=pltpu.CompilerParams(
            collective_id=0, has_side_effects=True, vmem_limit_bytes=67_000_000
        ),
    )(
        forward_sent[0],
        backward_sent[0],
        backward_routes[0].T,
        loss_gradient,
        forward_routes[0].T,
        embedded,
        norm_gain,
        router[0].T,
        down_weight[0],
        saved_pre,
        up_weight[0],
        saved_inputs[0],
    )
    return (forward_output[None], input_gradient[None])


def solution(mesh):
    return jax.shard_map(
        on_device,
        mesh=mesh,
        in_specs=(
            P("section", "expert", None),
            P("expert", None),
            P("section", "expert", None),
            P("section", "expert", None),
            P("expert", None),
            P("section", "expert", None),
            P("section", "expert", None),
            P("section", None, "expert", None, None),
            P("section", None),
            P("section", None, None),
            P("expert", None, None),
            P("expert", None, None),
        ),
        out_specs=(P("section", "expert", None), P("section", "expert", None)),
        check_vma=False,
    )
```

```python
import functools

import jax
import jax.numpy as jnp
from jax import lax
from jax.experimental import pallas as pl
from jax.experimental.pallas import tpu as pltpu
from jax.sharding import PartitionSpec as P

EPS = 1e-06
HIGH = lax.Precision.HIGHEST
LANE = 128
TILE = 256
GROUP = 32


def iota(shape, axis):
    return lax.broadcasted_iota(jnp.int32, shape, axis)


def onehot(condition):
    return jnp.where(condition, 1.0, 0.0).astype(jnp.bfloat16)


def dot(left, right, precision=None):
    return jnp.dot(
        left, right, preferred_element_type=jnp.float32, precision=precision
    )


def dot_transposed(left, right, precision=None):
    return lax.dot_general(
        left,
        right,
        (((1,), (1,)), ((), ())),
        preferred_element_type=jnp.float32,
        precision=precision,
    )


def columns(number):
    return pl.ds(pl.multiple_of(number * TILE, TILE), TILE)


def relay_kernel(
    sizes,
    forward_hbm,
    backward_hbm,
    routes_b_hbm,
    loss_hbm,
    routes_f_hbm,
    embedded_hbm,
    gain_hbm,
    router_hbm,
    down_hbm,
    pre_hbm,
    up_hbm,
    saved_hbm,
    out_f,
    out_b,
    routes_b,
    loss,
    routes_f,
    embedded,
    gain,
    router,
    down,
    pre,
    up,
    saved,
    arrived,
    returned,
    tokens,
    upstream,
    normed,
    mixing,
    gained,
    send_f,
    send_b,
    got_f,
    got_b,
    ret_f,
    ret_b,
    back_f,
    back_b,
    ret_s,
    back_s,
    wide,
    mid,
    load_sem,
    send_sem,
    recv_sem,
    pass_send,
    pass_recv,
):
    devices, sections, experts, capacity = sizes
    section = lax.axis_index("section")
    me = lax.axis_index("expert")
    chips = devices // 2
    spot, core = me // 2, lax.rem(me, 2)
    hidden_size, width = down.shape
    count = tokens.shape[0]
    rows = experts * capacity
    sub = width // LANE
    entry = capacity * sub

    barrier = pltpu.get_barrier_semaphore()
    ahead = {"section": lax.rem(section + 1, sections)}
    behind = {"section": lax.rem(section + sections - 1, sections)}
    pl.semaphore_signal(barrier, 1, device_id=ahead)
    pl.semaphore_signal(barrier, 1, device_id=behind)

    @pl.loop(1, devices)
    def _(step):
        pl.semaphore_signal(
            barrier, 1, device_id={"expert": lax.rem(me + step, devices)}
        )

    pairs = (
        (routes_b_hbm, routes_b),
        (loss_hbm, loss),
        (routes_f_hbm, routes_f),
        (embedded_hbm, embedded),
        (gain_hbm, gain),
        (router_hbm, router),
        (down_hbm, down),
        (pre_hbm, pre),
        (up_hbm, up),
        (saved_hbm, saved),
    )
    loads = [
        pltpu.make_async_copy(source, target, load_sem.at[number])
        for number, (source, target) in enumerate(pairs)
    ]
    for load in loads:
        load.start()

    def peer_of(number):
        place = number + 2
        distance = chips // 2 - place // 4
        way = 2 * lax.rem(place // 2, 2) - 1
        spot_there = lax.rem(spot + way * distance + chips, chips)
        return spot_there * 2 + lax.rem(core + number, 2)

    def part(ref, device):
        return ref.at[pl.ds(pl.multiple_of(device * entry, entry), entry), :]

    def copy_of(stage, number, peer, source, target):
        if stage < 4:
            here, there = part(source, peer), part(target, me)
        else:
            here, there = source.at[peer], target.at[me]
        return pltpu.make_async_remote_copy(
            src_ref=here,
            dst_ref=there,
            send_sem=send_sem.at[stage, number],
            recv_sem=recv_sem.at[stage, number],
            device_id={"expert": peer},
        )

    partner = spot * 2 + 1 - core

    def for_peers(act):
        @pl.loop(0, devices - 2)
        def _(number):
            act(number, peer_of(number))

        act(devices - 2, partner)

    def exchange(stage, source, target):
        for_peers(
            lambda number, peer: copy_of(stage, number, peer, source, target).start()
        )
        if stage < 4:
            own = pl.ds(pl.multiple_of(me * entry, entry), entry)
            target[own, :] = source[own, :]
        else:
            target[me] = source[me]

    def arrive(stage, source, target):
        for_peers(
            lambda number, _: copy_of(
                stage, number, partner, source, target
            ).wait_recv()
        )

    def leave(stage, source, target):
        for_peers(
            lambda number, _: copy_of(
                stage, number, partner, source, target
            ).wait_send()
        )

    side = GROUP * sub
    to_wide = onehot(
        iota((side, side), 1)
        == lax.rem(iota((side, side), 0), GROUP) * sub + iota((side, side), 0) // GROUP
    )
    to_lanes = onehot(
        iota((side, side), 0)
        == lax.rem(iota((side, side), 1), GROUP) * sub + iota((side, side), 1) // GROUP
    )

    def widen(source):
        @pl.loop(0, rows // GROUP)
        def _(number):
            block = source[pl.ds(pl.multiple_of(number * side, side), side), :]
            moved = dot(to_wide, block).astype(jnp.bfloat16)
            here = pl.ds(pl.multiple_of(number * GROUP, GROUP), GROUP)
            for k in range(sub):
                wide[here, k * LANE : (k + 1) * LANE] = moved[
                    k * GROUP : (k + 1) * GROUP, :
                ]

    def narrow(target):
        @pl.loop(0, rows // GROUP)
        def _(number):
            here = pl.ds(pl.multiple_of(number * GROUP, GROUP), GROUP)
            block = jnp.concatenate(
                [wide[here, k * LANE : (k + 1) * LANE] for k in range(sub)], axis=0
            )
            target[pl.ds(pl.multiple_of(number * side, side), side), :] = dot(
                to_lanes, block
            ).astype(jnp.bfloat16)

    earlier = onehot(iota((count, count), 0) < iota((count, count), 1))
    identity = onehot(iota((count, count), 0) == iota((count, count), 1))

    def follow(routes):
        named = [routes[k : k + 1, :] for k in range(routes.shape[0])]
        hits = [iota((experts, count), 0) == name for name in named]
        chosen = onehot(hits[0])
        for hit in hits[1:]:
            chosen = chosen + onehot(hit)
        before = dot(chosen, earlier)
        ranks = [
            jnp.sum(jnp.where(hit, before, 0.0), axis=0, keepdims=True) for hit in hits
        ]
        slot_number = iota((rows, count), 0).astype(jnp.float32)
        places = [
            slot_number == name.astype(jnp.float32) * capacity + rank
            for name, rank in zip(named, ranks)
        ]
        return hits, ranks, places

    def dispatch(places, source, target):
        placing = onehot(places[0])
        for place in places[1:]:
            placing = placing + onehot(place)

        @pl.loop(0, width // TILE)
        def _(number):
            wide[:, columns(number)] = dot(
                placing, source[:, columns(number)]
            ).astype(jnp.bfloat16)

        narrow(target)

    def normalise(source):
        def add(number, total):
            value = source[:, columns(number)].astype(jnp.float32)
            return total + jnp.sum(value * value, axis=1, keepdims=True)

        total = lax.fori_loop(
            0, width // TILE, add, jnp.zeros((count, 1), jnp.float32)
        )
        inv_rms = lax.rsqrt(total / width + EPS)

        @pl.loop(0, width // TILE)
        def _(number):
            value = source[:, columns(number)].astype(jnp.float32)
            scale = gain[:, columns(number)].astype(jnp.float32)
            normed[:, columns(number)] = (value * inv_rms * scale).astype(jnp.bfloat16)

        return inv_rms

    def share(hits, places):
        logits = dot_transposed(router[...], normed[...])
        powers = [
            jnp.exp(jnp.sum(jnp.where(hit, logits, 0.0), axis=0, keepdims=True))
            for hit in hits
        ]
        whole = powers[0]
        for power in powers[1:]:
            whole = whole + power
        shares = [power / whole for power in powers]
        mixed = jnp.zeros((rows, count), jnp.float32)
        for portion, place in zip(shares, places):
            rounded = portion.astype(jnp.bfloat16).astype(jnp.float32)
            mixed = mixed + jnp.where(place, rounded, 0.0)
        mixed = dot_transposed(identity, mixed.astype(jnp.bfloat16))
        return shares, mixed.astype(jnp.bfloat16)

    for load in loads[:2]:
        load.wait()
    hits_b, ranks_b, places_b = follow(routes_b)
    pl.semaphore_wait(barrier, devices + 1)
    pass_back = pltpu.make_async_remote_copy(
        src_ref=backward_hbm,
        dst_ref=returned,
        send_sem=pass_send.at[0],
        recv_sem=pass_recv.at[0],
        device_id=behind,
    )
    pass_on = pltpu.make_async_remote_copy(
        src_ref=forward_hbm,
        dst_ref=arrived,
        send_sem=pass_send.at[1],
        recv_sem=pass_recv.at[1],
        device_id=ahead,
    )
    pass_back.start()
    pass_on.start()
    pass_back.wait_recv()
    upstream[...] = jnp.where(section == sections - 1, loss[...], returned[...])
    dispatch(places_b, upstream, send_b)
    exchange(0, send_b, got_b)

    for load in loads[2:6]:
        load.wait()
    hits_f, _, places_f = follow(routes_f)
    pass_on.wait_recv()
    tokens[...] = jnp.where(section == 0, embedded[...], arrived[...])
    normalise(tokens)
    dispatch(places_f, normed, send_f)
    exchange(1, send_f, got_f)
    mixing[...] = share(hits_f, places_f)[1]

    for load in loads[6:]:
        load.wait()
    arrive(0, send_b, got_b)
    widen(got_b)
    pick = onehot(
        iota((rows, rows), 1)
        == lax.rem(iota((rows, rows), 0), capacity) * devices
        + iota((rows, rows), 0) // capacity
    )

    def back_tile(number, inner):
        grad = dot_transposed(wide[...], down[columns(number), :])
        value = dot(pick, pre[:, columns(number)])
        gate = jax.nn.sigmoid(value)
        rounded = (value * gate).astype(jnp.bfloat16).astype(jnp.float32)
        mid[:, columns(number)] = (
            grad * gate * (1.0 + value * (1.0 - gate))
        ).astype(jnp.bfloat16)
        return inner + jnp.sum(grad * rounded, axis=1, keepdims=True)

    inner = lax.fori_loop(
        0, hidden_size // TILE, back_tile, jnp.zeros((rows, 1), jnp.float32)
    )
    spread = jnp.where(
        iota((rows, LANE), 1) == lax.rem(iota((rows, LANE), 0), capacity), inner, 0.0
    ).astype(jnp.bfloat16)
    gather = onehot(iota((devices, rows), 0) == iota((devices, rows), 1) // capacity)
    sums = dot(gather, spread)
    for number in range(devices):
        ret_s[number] = sums[number : number + 1, :]

    @pl.loop(0, width // TILE)
    def _(number):
        wide[:, columns(number)] = dot_transposed(
            mid[...], up[columns(number), :]
        ).astype(jnp.bfloat16)

    narrow(ret_b)
    exchange(4, ret_s, back_s)
    exchange(2, ret_b, back_b)

    arrive(1, send_f, got_f)
    widen(got_f)

    @pl.loop(0, hidden_size // TILE)
    def _(number):
        value = dot(wide[...], up[:, columns(number)])
        mid[:, columns(number)] = jax.nn.silu(value).astype(jnp.bfloat16)

    @pl.loop(0, width // TILE)
    def _(number):
        wide[:, columns(number)] = dot(mid[...], down[:, columns(number)]).astype(
            jnp.bfloat16
        )

    narrow(ret_f)
    exchange(3, ret_f, back_f)

    pass_back.wait_send()
    pass_on.wait_send()
    leave(0, send_b, got_b)
    leave(1, send_f, got_f)
    inv_rms = normalise(saved)
    shares_b, mixed_b = share(hits_b, places_b)
    arrive(4, ret_s, back_s)
    table = jnp.concatenate([back_s[number] for number in range(experts)], axis=0)
    totals = []
    for hit, rank in zip(hits_b, ranks_b):
        total = jnp.zeros((1, count), jnp.float32)
        for slot in range(capacity):
            named = jnp.sum(
                jnp.where(hit, table[:, slot : slot + 1], 0.0), axis=0, keepdims=True
            )
            total = total + jnp.where(rank == slot, named, 0.0)
        totals.append(total)
    whole = shares_b[0] * totals[0]
    for portion, total in zip(shares_b[1:], totals[1:]):
        whole = whole + portion * total
    logit_grad = jnp.zeros((experts, count), jnp.float32)
    for hit, portion, total in zip(hits_b, shares_b, totals):
        logit_grad = logit_grad + jnp.where(hit, portion * (total - whole), 0.0)
    logit_grad = dot_transposed(identity.astype(jnp.float32), logit_grad, HIGH)
    arrive(2, ret_b, back_b)
    widen(back_b)

    def grad_tile(number, total):
        grad = dot(mixed_b, wide[:, columns(number)]) + dot(
            logit_grad, router[:, columns(number)].astype(jnp.float32), HIGH
        )
        grad = grad * gain[:, columns(number)].astype(jnp.float32)
        gained[:, columns(number)] = grad
        value = saved[:, columns(number)].astype(jnp.float32)
        return total + jnp.sum(value * grad, axis=1, keepdims=True)

    total = lax.fori_loop(
        0, width // TILE, grad_tile, jnp.zeros((count, 1), jnp.float32)
    )
    along = inv_rms * inv_rms * inv_rms * (total / width)

    @pl.loop(0, width // TILE)
    def _(number):
        value = saved[:, columns(number)].astype(jnp.float32)
        grad = inv_rms * gained[:, columns(number)] - value * along
        out_b[:, columns(number)] = (
            upstream[:, columns(number)].astype(jnp.float32) + grad
        ).astype(jnp.bfloat16)

    leave(4, ret_s, back_s)
    leave(2, ret_b, back_b)
    arrive(3, ret_f, back_f)
    widen(back_f)

    @pl.loop(0, width // TILE)
    def _(number):
        value = tokens[:, columns(number)].astype(jnp.float32)
        out_f[:, columns(number)] = (
            value + dot(mixing[...], wide[:, columns(number)])
        ).astype(jnp.bfloat16)

    leave(3, ret_f, back_f)


def on_device(
    forward_sent,
    embedded,
    forward_routes,
    backward_sent,
    loss_gradient,
    saved_inputs,
    backward_routes,
    pre_activation,
    norm_gain,
    router,
    up_weight,
    down_weight,
):
    devices = lax.axis_size("expert")
    sections = lax.axis_size("section")
    experts = router.shape[2]
    capacity = pre_activation.shape[3]
    count, width = embedded.shape
    hidden_size = up_weight.shape[2]
    slots = experts * capacity
    saved_pre = pre_activation[0, :, 0].transpose(1, 0, 2).reshape(slots, hidden_size)
    vmem = pl.BlockSpec(memory_space=pltpu.VMEM)
    hbm = pl.BlockSpec(memory_space=pltpu.HBM)
    block = jax.ShapeDtypeStruct((count, width), jnp.bfloat16)
    held = pltpu.VMEM((count, width), jnp.bfloat16)
    lanes = pltpu.VMEM((slots * width // LANE, LANE), jnp.bfloat16)
    small = pltpu.VMEM((devices, 1, LANE), jnp.float32)
    forward_output, input_gradient = pl.pallas_call(
        functools.partial(relay_kernel, (devices, sections, experts, capacity)),
        out_shape=(block, block),
        in_specs=[hbm] * 12,
        out_specs=(vmem, vmem),
        scratch_shapes=[
            pltpu.VMEM(forward_routes.shape[:0:-1], jnp.int32),
            held,
            pltpu.VMEM(forward_routes.shape[:0:-1], jnp.int32),
            held,
            pltpu.VMEM((1, width), jnp.bfloat16),
            pltpu.VMEM((experts, width), jnp.bfloat16),
            pltpu.VMEM((hidden_size, width), jnp.bfloat16),
            pltpu.VMEM((slots, hidden_size), jnp.bfloat16),
            pltpu.VMEM((width, hidden_size), jnp.bfloat16),
            held,
            held,
            held,
            held,
            held,
            held,
            pltpu.VMEM((count, slots), jnp.bfloat16),
            pltpu.VMEM((count, width), jnp.float32),
            *[lanes] * 8,
            small,
            small,
            pltpu.VMEM((slots, width), jnp.bfloat16),
            pltpu.VMEM((slots, hidden_size), jnp.bfloat16),
            pltpu.SemaphoreType.DMA((10,)),
            pltpu.SemaphoreType.DMA((5, devices)),
            pltpu.SemaphoreType.DMA((5, devices)),
            pltpu.SemaphoreType.DMA((2,)),
            pltpu.SemaphoreType.DMA((2,)),
        ],
        compiler_params=pltpu.CompilerParams(
            collective_id=0, has_side_effects=True, vmem_limit_bytes=67_000_000
        ),
    )(
        forward_sent[0],
        backward_sent[0],
        backward_routes[0].T,
        loss_gradient,
        forward_routes[0].T,
        embedded,
        norm_gain,
        router[0].T,
        down_weight[0],
        saved_pre,
        up_weight[0],
        saved_inputs[0],
    )
    return (forward_output[None], input_gradient[None])


def solution(mesh):
    return jax.shard_map(
        on_device,
        mesh=mesh,
        in_specs=(
            P("section", "expert", None),
            P("expert", None),
            P("section", "expert", None),
            P("section", "expert", None),
            P("expert", None),
            P("section", "expert", None),
            P("section", "expert", None),
            P("section", None, "expert", None, None),
            P("section", None),
            P("section", None, None),
            P("expert", None, None),
            P("expert", None, None),
        ),
        out_specs=(P("section", "expert", None), P("section", "expert", None)),
        check_vma=False,
    )
```
